256 devices in a mesh: dom: 64 (over z, y, core), grp: 4 (over x).
Axes of the slice: x: 4, y: 4, z: 8, core: 2. Of those that a mesh axis runs over, the one named last changes fastest.
Arguments:
- features: bfloat16 [4, 65536, 512], P('grp', 'dom'), may hold values from -6 to 6
- history: bfloat16 [2, 4, 65536, 512], P(None, 'grp', 'dom'), may hold values from -6 to 6
- adj_tiles: bfloat16 [4, 512, 4, 128, 128], P('grp', 'dom'), may hold values from -0.25 to 0.25
- blocks: int32 [4, 512, 4], P('grp', 'dom'), may hold values from 0 to 11, as said below
- send_list: int32 [4, 64, 64, 8], P('grp', 'dom'), may hold values from 0 to 1023
- counts: int32 [4, 64, 64], P('grp', 'dom'), may hold values from 0 to 8, as said below
- weights: bfloat16 [3, 512, 512], replicated, may hold values from -0.25 to 0.25
- cotangent: bfloat16 [4, 65536, 512], P('grp', 'dom'), may hold values from -16 to 16
Outputs:
- embedding: bfloat16 [4, 65536, 512], P('grp', 'dom')
- fresh_halo: bfloat16 [2, 4, 32768, 512], P(None, 'grp', 'dom')
- weight_grads: float32 [3, 512, 512], P(None, 'dom')
The draws below stay inside these ranges and needn't reach their ends.
Inputs may be any that keep to these rules, and one draw needn't show every extreme that they name: `send_list`: entries at or past counts are not read. counts[g, q, p] is zero where q equals p; some owner uses all 8 slots for every other partition, and some partition gets 8 rows from every other owner. Entry 0 of the list of a partition's block b is b itself; entries 2 and 3 name halo blocks, at least 8.
All inputs are finite; a program needn't handle non-finite values.
Results may differ from the reference program's by a relative error of at most 0.012.
Values may be sent and summed in bfloat16 or wider, within the bound.
A program may use at most 128 MiB of HBM per device.

```python
import math
import jax
import jax.numpy as jnp
from jax import lax

D = 512
LAYERS = 3
BLK = 128
K = 4
P_SIZE = 1024
HALO = 512
CAP = 8
NODES = 65536
N_DOM = 64
N_GRP = 4


def draw_counts(key, part):
    key_light, key_owner, key_recv, key_first, key_second = jax.random.split(key, 5)
    position = jnp.arange(N_DOM, dtype=jnp.int32)
    heavy_owner = jax.random.randint(key_owner, (N_GRP, N_DOM), 0, 4) == 0
    heavy_recv = jax.random.randint(key_recv, (N_GRP, N_DOM), 0, 4) == 0
    forced_owner = jax.random.randint(key_first, (N_GRP,), 0, N_DOM)
    forced_recv = jax.random.randint(key_second, (N_GRP,), 0, N_DOM)
    heavy_owner = heavy_owner | (position[None, :] == forced_owner[:, None])
    heavy_recv = heavy_recv | (position[None, :] == forced_recv[:, None])
    light = jax.random.randint(key_light, (N_GRP, N_DOM, N_DOM), 0, CAP // 2 + 1)
    filled = heavy_owner[:, :, None] | heavy_recv[:, None, :]
    result = jnp.where(filled, CAP, light)
    result = jnp.where((position[:, None] == position[None, :])[None, :, :], 0, result)
    return result.astype(jnp.int32)


def draw_blocks(key, part):
    local_count = P_SIZE // BLK
    halo_count = HALO // BLK
    key_local, key_offset = jax.random.split(key, 2)
    own_block = jnp.broadcast_to(jnp.arange(local_count, dtype=jnp.int32)[None, None, :], (N_GRP, N_DOM, local_count))
    local_pick = jax.random.randint(key_local, (N_GRP, N_DOM, local_count), 0, local_count)
    offset = jax.random.randint(key_offset, (N_GRP, N_DOM, 1), 0, halo_count)
    halo_first = local_count + (2 * own_block + offset) % halo_count
    halo_second = local_count + (2 * own_block + 1 + offset) % halo_count
    stacked = jnp.stack([own_block, local_pick, halo_first, halo_second], axis=-1)
    return stacked.reshape(N_GRP, N_DOM * local_count, 4).astype(jnp.int32)


def place_ends(drawn, rng, least, top_value):
    index_at = [jax.random.randint(jax.random.fold_in(rng, axis), (), 0, length) for axis, length in enumerate(drawn.shape)]
    main_axis = drawn.shape.index(max(drawn.shape))
    next_to = index_at[:main_axis] + [(index_at[main_axis] + 1) % drawn.shape[main_axis]] + index_at[main_axis + 1:]
    return drawn.at[tuple(index_at)].set(least).at[tuple(next_to)].set(top_value)


def with_spikes(entries, rng, source, target, shards_of, factor):
    def block_of(axis_at):
        return (jnp.arange(entries.shape[axis_at]) // (entries.shape[axis_at] // shards_of)).reshape((-1,) + (1,) * (entries.ndim - 1 - axis_at))

    one_side = jax.random.permutation(rng, shards_of)[block_of(target)]
    far = (block_of(target) + shards_of // 2) % shards_of
    return jnp.where((block_of(source) == one_side) | (block_of(source) == far), factor * entries, entries)


def level_of(rng, extent, shards, low, largest):
    gain = 1.0
    for axis_at, shards_of in shards:
        draws = jax.random.uniform(jax.random.fold_in(jax.random.fold_in(rng, 6), axis_at), (shards_of,), jnp.float32, low / len(shards), largest / len(shards))
        gain = gain * jnp.repeat(jnp.exp(draws), extent[axis_at] // shards_of).reshape((-1,) + (1,) * (len(extent) - 1 - axis_at))
    return gain


def noise(key, extent, width, bound, shards=(), kind=jnp.bfloat16):
    array = width * jax.random.normal(key, extent, jnp.float32)
    if shards:
        array = array * level_of(key, extent, shards, -0.22, 0.18)
    return jnp.clip(array, -bound, bound).astype(kind)


def noise_with(own_key, shape, spread, reach, pieces, heavy, held_as=jnp.bfloat16):
    drawn = spread * jax.random.normal(own_key, shape, jnp.float32)
    if pieces:
        drawn = drawn * level_of(own_key, shape, pieces, -0.22, 0.18)
    return jnp.clip(with_spikes(drawn, jax.random.fold_in(own_key, 3), *heavy), -reach, reach).astype(held_as)


def setup_inputs(seed: int = 0) -> dict:
    seeds = jax.random.split(jax.random.key(seed), 9)
    return {
        "features": noise(seeds[0], (N_GRP, NODES, D), 1.0, 6.0, ((0, 4), (1, 64))),
        "history": noise(seeds[1], (LAYERS - 1, N_GRP, NODES, D), 1.0, 6.0, ((1, 4), (2, 64))),
        "adj_tiles": noise(seeds[2], (N_GRP, NODES // BLK, K, BLK, BLK), (K * BLK) ** -0.5, 0.25, ((0, 4), (1, 64))),
        "blocks": draw_blocks(jax.random.fold_in(seeds[8], 71), 0),
        "send_list": place_ends(jax.random.randint(seeds[4], (N_GRP, N_DOM, N_DOM, CAP), 0, P_SIZE), jax.random.fold_in(seeds[4], 1), 0, P_SIZE - 1).astype(jnp.int32),
        "counts": draw_counts(jax.random.fold_in(seeds[8], 71), 0),
        "weights": noise(seeds[6], (LAYERS, D, D), D ** -0.5, 0.25),
        "cotangent": noise_with(seeds[7], (N_GRP, NODES, D), 1.0, 16.0, ((0, 4), (1, 64)), (1, 2, 64, 4.0)),
    }


def silu_slope(values):
    sigmoid_part = jax.nn.sigmoid(values)
    return sigmoid_part * (1.0 + values * (1.0 - sigmoid_part))

def take_rows(table_rows, row_index):
    return jnp.take(table_rows, row_index, axis=0)

def pull_rows(source_rows, send_list, counts):
    groups = send_list.shape[0]
    owners_count = send_list.shape[1]
    capacity = send_list.shape[3]
    part_rows = source_rows.shape[1] // owners_count
    offset = (jnp.arange(owners_count, dtype=jnp.int32) * part_rows)[None, :, None, None]
    row_index = jnp.transpose(send_list + offset, (0, 2, 1, 3)).reshape(groups, -1)
    in_use = jnp.arange(capacity, dtype=jnp.int32)[None, None, None, :] < counts[:, :, :, None]
    in_use = jnp.transpose(in_use, (0, 2, 1, 3)).reshape(groups, -1)
    picked = jax.vmap(take_rows)(source_rows, row_index)
    return jnp.where(in_use[:, :, None], picked, jnp.zeros((), source_rows.dtype))

def aggregate_one(operands):
    local_rows, halo_rows, tile_set, block_set = operands
    row_width = local_rows.shape[1]
    block_rows = tile_set.shape[-1]
    source = jnp.concatenate([local_rows, halo_rows], axis=0).reshape(-1, block_rows, row_width)
    picked = jnp.take(source, block_set.reshape(-1).astype(jnp.int32), axis=0)
    picked = picked.reshape(block_set.shape + (block_rows, row_width))
    mixed = jnp.einsum('bkij,bkjd->bid', tile_set.astype(jnp.float32), picked.astype(jnp.float32), precision=lax.Precision.HIGHEST)
    return mixed.reshape(-1, row_width).astype(jnp.bfloat16)

def spread_one(operands):
    grad_rows, tile_set, block_set = operands
    row_width = grad_rows.shape[1]
    block_rows = tile_set.shape[-1]
    local_blocks = grad_rows.shape[0] // block_rows
    by_block = grad_rows.reshape(-1, block_rows, row_width)
    contrib_terms = jnp.einsum('bkij,bid->bkjd', tile_set.astype(jnp.float32), by_block.astype(jnp.float32), precision=lax.Precision.HIGHEST)
    owners = (block_set.reshape(1, -1) == jnp.arange(local_blocks, dtype=jnp.int32)[:, None]).astype(jnp.float32)
    summed = jnp.dot(owners, contrib_terms.reshape(owners.shape[1], -1), precision=lax.Precision.HIGHEST, preferred_element_type=jnp.float32)
    return summed.reshape(-1, row_width)

def reference(features, history, adj_tiles, blocks, send_list, counts, weights, cotangent):
    groups = counts.shape[0]
    owners_count = counts.shape[1]
    devices = groups * owners_count
    row_width = features.shape[2]
    part_rows = features.shape[1] // owners_count
    tile_dev = adj_tiles.reshape((devices, -1) + adj_tiles.shape[2:])
    block_dev = blocks.reshape(devices, -1, blocks.shape[2])
    halo_inputs = [pull_rows(features, send_list, counts), pull_rows(history[0], send_list, counts), pull_rows(history[1], send_list, counts)]
    current = features
    aggregated = []
    linear_out = []
    hidden_rows = []
    for layer_index in range(3):
        mixed = lax.map(aggregate_one, (current.reshape(devices, part_rows, row_width), halo_inputs[layer_index].reshape(devices, -1, row_width), tile_dev, block_dev))
        mixed = mixed.reshape(-1, row_width)
        product = jnp.dot(mixed, weights[layer_index], preferred_element_type=jnp.float32)
        aggregated.append(mixed)
        linear_out.append(product)
        if layer_index < 2:
            current = jax.nn.silu(product).astype(jnp.bfloat16).reshape(features.shape)
            hidden_rows.append(current)
    embedding = linear_out[2].astype(jnp.bfloat16).reshape(features.shape)
    fresh_halo = jnp.stack([pull_rows(hidden_rows[0], send_list, counts), pull_rows(hidden_rows[1], send_list, counts)])
    upstream = cotangent.reshape(-1, row_width)
    partial_sums = [None, None, None]
    for layer_index in (2, 1, 0):
        partial_sums[layer_index] = jnp.dot(aggregated[layer_index].T, upstream, preferred_element_type=jnp.float32)
        if layer_index > 0:
            slope_in = jnp.dot(upstream, weights[layer_index].T, preferred_element_type=jnp.float32).astype(jnp.bfloat16)
            back_rows = lax.map(spread_one, (slope_in.reshape(devices, part_rows, row_width), tile_dev, block_dev)).reshape(-1, row_width)
            upstream = (back_rows * silu_slope(linear_out[layer_index - 1])).astype(jnp.bfloat16)
    weight_grads = jnp.stack(partial_sums) * (1.0 / math.sqrt(groups * features.shape[1]))
    return (embedding, fresh_halo, weight_grads)
```

```python
import math

import jax
import jax.numpy as jnp
from jax import lax
from jax.sharding import PartitionSpec as P


def silu_slope(values):
    sigmoid_part = jax.nn.sigmoid(values)
    return sigmoid_part * (1.0 + values * (1.0 - sigmoid_part))


def pack_rows(source_rows, send_rows, live_counts):
    peer_count = send_rows.shape[0]
    capacity = send_rows.shape[1]
    picked = jnp.take(source_rows, send_rows.reshape(-1), axis=0)
    picked = picked.reshape(peer_count, capacity, source_rows.shape[1])
    in_use = jnp.arange(capacity, dtype=jnp.int32)[None, :] < live_counts[:, None]
    return jnp.where(in_use[:, :, None], picked, jnp.zeros((), jnp.bfloat16))


def aggregate(local_rows, halo_rows, tile_set, block_set):
    block_rows = tile_set.shape[-1]
    row_width = local_rows.shape[1]
    source = jnp.concatenate([local_rows, halo_rows], axis=0).reshape(-1, block_rows, row_width)
    picked = jnp.take(source, block_set.reshape(-1), axis=0)
    picked = picked.reshape(block_set.shape + (block_rows, row_width))
    mixed = jnp.einsum("bkij,bkjd->bid", tile_set, picked, preferred_element_type=jnp.float32)
    return mixed.reshape(-1, row_width)


def spread_back(grad_rows, tile_set, block_set):
    block_rows = tile_set.shape[-1]
    row_width = grad_rows.shape[1]
    local_blocks = grad_rows.shape[0] // block_rows
    by_block = grad_rows.reshape(-1, block_rows, row_width)
    contrib_terms = jnp.einsum(
        "bkij,bid->bkjd", tile_set, by_block, preferred_element_type=jnp.float32
    )
    owners = (
        block_set.reshape(1, -1) == jnp.arange(local_blocks, dtype=jnp.int32)[:, None]
    ).astype(jnp.float32)
    summed = jnp.dot(
        owners,
        contrib_terms.reshape(owners.shape[1], -1),
        precision=lax.Precision.HIGHEST,
        preferred_element_type=jnp.float32,
    )
    return summed.reshape(-1, row_width)


def body(features, history, adj_tiles, blocks, send_list, counts, weights, cotangent):
    node_rows = features[0]
    tile_set = adj_tiles[0]
    block_set = blocks[0]
    send_rows = send_list[0, 0]
    live_counts = counts[0, 0]
    row_width = node_rows.shape[1]
    pulled = (
        lax.all_to_all(
            pack_rows(node_rows, send_rows, live_counts),
            "dom",
            split_axis=0,
            concat_axis=0,
            tiled=True,
        ),
        lax.all_to_all(
            pack_rows(history[0, 0], send_rows, live_counts),
            "dom",
            split_axis=0,
            concat_axis=0,
            tiled=True,
        ),
        lax.all_to_all(
            pack_rows(history[1, 0], send_rows, live_counts),
            "dom",
            split_axis=0,
            concat_axis=0,
            tiled=True,
        ),
    )
    halo_inputs = [piece.reshape(-1, row_width) for piece in pulled]
    current = node_rows
    aggregated = []
    linear_out = []
    hidden_rows = []
    fresh_parts = []
    for layer_index in range(3):
        mixed = aggregate(current, halo_inputs[layer_index], tile_set, block_set).astype(
            jnp.bfloat16
        )
        product = jnp.dot(mixed, weights[layer_index], preferred_element_type=jnp.float32)
        aggregated.append(mixed)
        linear_out.append(product)
        if layer_index < 2:
            current = jax.nn.silu(product).astype(jnp.bfloat16)
            hidden_rows.append(current)
    node_out = linear_out[2].astype(jnp.bfloat16)
    fresh_parts = list(
        (
            lax.all_to_all(
                pack_rows(hidden_rows[0], send_rows, live_counts),
                "dom",
                split_axis=0,
                concat_axis=0,
                tiled=True,
            ),
            lax.all_to_all(
                pack_rows(hidden_rows[1], send_rows, live_counts),
                "dom",
                split_axis=0,
                concat_axis=0,
                tiled=True,
            ),
        )
    )
    fresh_halo = jnp.stack([piece.reshape(-1, row_width) for piece in fresh_parts])
    upstream = cotangent[0]
    partial_sums = [None, None, None]
    for layer_index in (2, 1, 0):
        partial_sums[layer_index] = lax.dot_general(
            aggregated[layer_index],
            upstream,
            (((0,), (0,)), ((), ())),
            preferred_element_type=jnp.float32,
        )
        if layer_index > 0:
            slope_in = lax.dot_general(
                upstream,
                weights[layer_index],
                (((1,), (1,)), ((), ())),
                preferred_element_type=jnp.float32,
            ).astype(jnp.bfloat16)
            back_rows = spread_back(slope_in, tile_set, block_set)
            upstream = (back_rows * silu_slope(linear_out[layer_index - 1])).astype(jnp.bfloat16)
    total_rows = lax.axis_size("grp") * lax.axis_size("dom") * node_rows.shape[0]
    stacked = jnp.stack(partial_sums) * (1.0 / math.sqrt(total_rows))
    n_dom = lax.axis_size("dom")
    pieces = stacked.astype(jnp.bfloat16).reshape(3, n_dom, -1, row_width).transpose(1, 0, 2, 3)
    arrived = lax.all_to_all(pieces, "dom", split_axis=0, concat_axis=0, tiled=True)
    dom_total = jnp.sum(arrived.astype(jnp.float32), axis=0)
    weight_grads = lax.psum(dom_total, "grp")
    return (node_out[None], fresh_halo[:, None], weight_grads)


def solution(mesh):
    placed = (
        P("grp", "dom", None),
        P(None, "grp", "dom", None),
        P("grp", "dom", None, None, None),
        P("grp", "dom", None),
        P("grp", "dom", None, None),
        P("grp", "dom", None),
        P(),
        P("grp", "dom", None),
    )
    return jax.shard_map(
        body,
        mesh=mesh,
        in_specs=placed,
        out_specs=(P("grp", "dom", None), P(None, "grp", "dom", None), P(None, "dom", None)),
        check_vma=False,
    )
```

```python
import functools
import math

import jax
import jax.numpy as jnp
from jax import lax
from jax.experimental import pallas as pl
from jax.experimental.pallas import tpu as pltpu
from jax.sharding import PartitionSpec as P

MESH = pl.DeviceIdType.MESH
BF = jnp.bfloat16
F32 = jnp.float32
N_DOM, N_GRP, N_Z, N_Y = 64, 4, 8, 4
ROWS, D, HALO, CAP = 1024, 512, 512, 8
STEP = 256


def dot(a, b):
    return jnp.dot(a, b, preferred_element_type=F32)


def dot_rows(a, b):
    return lax.dot_general(a, b, (((0,), (0,)), ((), ())), preferred_element_type=F32)


def dot_t(a, b):
    return lax.dot_general(a, b, (((1,), (1,)), ((), ())), preferred_element_type=F32)


def step_kernel(
    blk, idx_h, feat_h, hist_h, adj_h, w_h, cot_h,
    emb_o, fresh_o, wg_o,
    idx, feat, hist, adj, w, cot, hot, mix, back_mix, halo, h1, h2, mid, slope0, slope1,
    dm, grad, acc, emb, send, recv,
    wg, core_in, x_out, x_in, y_out, y_in, z_out, z_in, quarters,
    in_sem, send_sem, recv_sem, core_sem, x_sem, y_sem, z_sem, q_sem, out_sem,
):
    me = lax.axis_index("dom")
    g = lax.axis_index("grp")
    z, y, c = me // 8, (me % 8) // 2, me % 2
    loads = [
        pltpu.make_async_copy(a, b, in_sem.at[i])
        for i, (a, b) in enumerate(
            [(idx_h, idx), (feat_h, feat), (hist_h.at[0], hist.at[0]), (hist_h.at[1], hist.at[1]),
             (adj_h, adj), (w_h, w), (cot_h, cot)]
        )
    ]
    for load in loads:
        load.start()

    barrier = pltpu.get_barrier_semaphore()

    def greet(s, _):
        pl.semaphore_signal(barrier, inc=1, device_id={"dom": lax.rem(me + s, N_DOM)}, device_id_type=MESH)
        return 0

    lax.fori_loop(1, N_DOM, greet, 0)
    for s in range(1, N_GRP):
        pl.semaphore_signal(barrier, inc=1, device_id={"grp": lax.rem(g + s, N_GRP)}, device_id_type=MESH)

    def gather(rows_ref, turn):
        def one(i, _):
            rows = pl.ds(pl.multiple_of(i * STEP, STEP), STEP)
            picked = dot(hot[rows, :], rows_ref[...])
            send[turn, pl.ds(i * (STEP // CAP), STEP // CAP)] = picked.reshape(STEP // CAP, CAP, D).astype(BF)
            return 0

        lax.fori_loop(0, HALO // STEP, one, 0)

    def exchange(turn):
        def one(s, _):
            half = (s + 1) // 2
            to = jnp.where(lax.rem(s, 2) == 1, lax.rem(me + half, N_DOM), lax.rem(me + N_DOM - half, N_DOM))
            pltpu.make_async_remote_copy(
                send.at[turn, to], recv.at[turn, me], send_sem.at[turn], recv_sem.at[turn],
                device_id={"dom": to}, device_id_type=MESH,
            ).start()
            return 0

        lax.fori_loop(1, N_DOM, one, 0)

    def arrived(turn):
        block = recv.at[turn, pl.ds(0, N_DOM - 1)]
        pltpu.make_async_copy(block, block, recv_sem.at[turn]).wait()

    def unpack(turn):
        def one(i, _):
            part = recv[turn, pl.ds(i * 8, 8)].astype(F32).reshape(64, D)
            halo[pl.ds(pl.multiple_of(i * 64, 64), 64), :] = part.astype(BF)
            return 0

        lax.fori_loop(0, N_DOM // 8, one, 0)

    def forward(layer, rows_ref, next_ref, slope_ref):
        def one(i, _):
            rows = pl.ds(pl.multiple_of(i * STEP, STEP), STEP)
            mixed = dot(mix[rows, 0:ROWS], rows_ref[...]) + dot(mix[rows, ROWS:ROWS + HALO], halo[...])
            mixed = mixed.astype(BF)
            mid[layer, rows, :] = mixed
            value = dot(mixed, w[layer])
            if slope_ref is None:
                next_ref[rows, :] = value.astype(BF)
            else:
                part = jax.nn.sigmoid(value)
                next_ref[rows, :] = (value * part).astype(BF)
                slope_ref[rows, :] = part * (1.0 + value * (1.0 - part))
            return 0

        lax.fori_loop(0, ROWS // STEP, one, 0)

    def back_through(layer, grad_ref):
        def one(i, _):
            rows = pl.ds(pl.multiple_of(i * STEP, STEP), STEP)
            dm[rows, :] = dot_t(grad_ref[rows, :], w[layer]).astype(BF)
            return 0

        lax.fori_loop(0, ROWS // STEP, one, 0)

    def spread(slope_ref):
        def one(i, _):
            rows = pl.ds(pl.multiple_of(i * STEP, STEP), STEP)
            grad[rows, :] = (dot(back_mix[rows, :], dm[...]) * slope_ref[rows, :]).astype(BF)
            return 0

        lax.fori_loop(0, ROWS // STEP, one, 0)

    def weight_grad(layer, grad_ref):
        acc[...] = jnp.zeros_like(acc)

        def one(i, _):
            rows = pl.ds(pl.multiple_of(i * STEP, STEP), STEP)
            acc[...] += dot_rows(mid[layer, rows, :], grad_ref[rows, :])
            return 0

        lax.fori_loop(0, ROWS // STEP, one, 0)
        wg[layer] = acc[...].reshape(32, 2, 8, D).astype(BF)
        core_copy(layer).start()

    def core_copy(layer):
        return pltpu.make_async_remote_copy(
            wg.at[layer, :, 1 - c], core_in.at[layer], core_sem.at[0, layer], core_sem.at[1, layer],
            device_id={"dom": me + 1 - 2 * c}, device_id_type=MESH,
        )

    def x_copy(layer, s):
        to = lax.rem(g + s, N_GRP)
        return pltpu.make_async_remote_copy(
            x_out.at[to, layer], x_in.at[s - 1, layer], x_sem.at[0, layer, s - 1], x_sem.at[1, layer, s - 1],
            device_id={"grp": to}, device_id_type=MESH,
        )

    def x_stage(layer):
        core_copy(layer).wait_recv()
        both = wg[layer, :, c].astype(F32) + core_in[layer].astype(F32)
        for q in range(N_GRP):
            x_out[q, layer] = both[:, :, q * 128:(q + 1) * 128].astype(BF)
        for s in range(1, N_GRP):
            x_copy(layer, s).start()

    def y_copy(s):
        to = lax.rem(y + s, N_Y)
        return pltpu.make_async_remote_copy(
            y_out.at[to], y_in.at[s - 1], y_sem.at[0, s - 1], y_sem.at[1, s - 1],
            device_id={"dom": z * 8 + to * 2 + c}, device_id_type=MESH,
        )

    def z_copy(s):
        to = lax.rem(z + s, N_Z)
        return pltpu.make_async_remote_copy(
            z_out.at[to], z_in.at[s - 1], z_sem.at[0, s - 1], z_sem.at[1, s - 1],
            device_id={"dom": to * 8 + y * 2 + c}, device_id_type=MESH,
        )

    def q_copy(s):
        return pltpu.make_async_remote_copy(
            quarters.at[g], quarters.at[g], q_sem.at[0, s - 1], q_sem.at[1, s - 1],
            device_id={"grp": lax.rem(g + s, N_GRP)}, device_id_type=MESH,
        )

    def y_prepare(layer):
        for s in range(1, N_GRP):
            x_copy(layer, s).wait_recv()
        total = x_out[g, layer].astype(F32)
        for s in range(1, N_GRP):
            total = total + x_in[s - 1, layer].astype(F32)
        total = total.reshape(N_Z, N_Y, 8, 128)
        for to in range(N_Y):
            y_out[to, layer] = total[:, to].astype(BF)

    loads[0].wait()
    lane = lax.broadcasted_iota(jnp.int32, (64, 128), 1)

    def mark(i, _):
        rows = pl.ds(pl.multiple_of(i * 64, 64), 64)
        wanted = idx[rows, :]
        for k in range(ROWS // 128):
            hot[rows, k * 128:(k + 1) * 128] = jnp.where(wanted == lane + k * 128, 1.0, 0.0).astype(BF)
        return 0

    lax.fori_loop(0, HALO // 64, mark, 0)
    loads[1].wait()
    gather(feat, 0)
    for turn in range(5):
        recv[turn, me] = jnp.zeros((CAP, D), BF)
    pl.semaphore_wait(barrier, N_DOM - 1 + N_GRP - 1)
    exchange(0)
    loads[2].wait()
    gather(hist.at[0], 1)
    exchange(1)
    loads[3].wait()
    gather(hist.at[1], 2)
    exchange(2)

    loads[4].wait()
    for b in range(8):
        tiles = [adj[b, k].astype(F32) for k in range(4)]
        rows = slice(b * 128, (b + 1) * 128)
        for j in range(12):
            if j < 8:
                entry = jnp.where(blk[b, 1] == j, tiles[1], 0.0)
                if j == b:
                    entry = entry + tiles[0]
            else:
                entry = jnp.where(blk[b, 1] == j, tiles[1], 0.0)
                entry = entry + jnp.where(blk[b, 2] == j, tiles[2], 0.0)
                entry = entry + jnp.where(blk[b, 3] == j, tiles[3], 0.0)
            mix[rows, j * 128:(j + 1) * 128] = entry.astype(BF)
            if j < 8:
                back_mix[j * 128:(j + 1) * 128, rows] = entry.T.astype(BF)

    loads[5].wait()
    loads[6].wait()
    back_through(2, cot)

    arrived(0)
    unpack(0)
    forward(0, feat, h1, slope0)
    gather(h1, 3)
    exchange(3)

    arrived(1)
    unpack(1)
    forward(1, h1, h2, slope1)
    gather(h2, 4)
    exchange(4)

    spread(slope1)
    weight_grad(1, grad)
    back_through(1, grad)
    spread(slope0)
    weight_grad(0, grad)
    x_stage(1)
    x_stage(0)

    arrived(2)
    unpack(2)
    forward(2, h2, emb, None)
    emb_copy = pltpu.make_async_copy(emb, emb_o, out_sem.at[0])
    emb_copy.start()
    weight_grad(2, cot)
    y_prepare(1)
    y_prepare(0)
    x_stage(2)
    y_prepare(2)
    for s in range(1, N_Y):
        y_copy(s).start()
    for s in range(1, N_Y):
        y_copy(s).wait_recv()
    total = y_out[y].astype(F32)
    for s in range(1, N_Y):
        total = total + y_in[s - 1].astype(F32)
    for to in range(N_Z):
        z_out[to] = total[:, to].astype(BF)
    for s in range(1, N_Z):
        z_copy(s).start()
    for s in range(1, N_Z):
        z_copy(s).wait_recv()
    total = z_out[z].astype(F32)
    for s in range(1, N_Z):
        total = total + z_in[s - 1].astype(F32)
    quarters[g] = total * (1.0 / math.sqrt(N_GRP * N_DOM * ROWS))
    for s in range(1, N_GRP):
        q_copy(s).start()

    fresh_copies = []
    for turn in (3, 4):
        arrived(turn)
        fresh_copies.append(pltpu.make_async_copy(recv.at[turn], fresh_o.at[turn - 3], out_sem.at[turn - 2]))
        fresh_copies[-1].start()
    for s in range(1, N_GRP):
        q_copy(s).wait_recv()
    for q in range(N_GRP):
        wg_o[:, :, q * 128:(q + 1) * 128] = quarters[q]

    for turn in range(5):
        block = send.at[turn, pl.ds(0, N_DOM - 1)]
        pltpu.make_async_copy(block, block, send_sem.at[turn]).wait()
    for layer in range(3):
        core_copy(layer).wait_send()
        for s in range(1, N_GRP):
            x_copy(layer, s).wait_send()
    for s in range(1, N_Y):
        y_copy(s).wait_send()
    for s in range(1, N_Z):
        z_copy(s).wait_send()
    for s in range(1, N_GRP):
        q_copy(s).wait_send()
    emb_copy.wait()
    for copy in fresh_copies:
        copy.wait()


def body(features, history, adj_tiles, blocks, send_list, counts, weights, cotangent):
    in_use = jnp.arange(CAP, dtype=jnp.int32)[None, :] < counts[0, 0][:, None]
    wanted = jnp.where(in_use, send_list[0, 0], -1).reshape(HALO, 1)
    wanted = jnp.broadcast_to(wanted, (HALO, 128))
    vmem = pltpu.VMEM
    dma = pltpu.SemaphoreType.DMA
    embedding, fresh, grads = pl.pallas_call(
        step_kernel,
        out_shape=(
            jax.ShapeDtypeStruct((ROWS, D), BF),
            jax.ShapeDtypeStruct((2, N_DOM, CAP, D), BF),
            jax.ShapeDtypeStruct((3, 8, D), F32),
        ),
        in_specs=[pl.BlockSpec(memory_space=pltpu.SMEM)] + [pl.BlockSpec(memory_space=pl.ANY)] * 6,
        out_specs=(
            pl.BlockSpec(memory_space=pl.ANY),
            pl.BlockSpec(memory_space=pl.ANY),
            pl.BlockSpec(memory_space=vmem),
        ),
        scratch_shapes=[
            vmem((HALO, 128), jnp.int32),
            vmem((ROWS, D), BF),
            vmem((2, ROWS, D), BF),
            vmem((8, 4, 128, 128), BF),
            vmem((3, D, D), BF),
            vmem((ROWS, D), BF),
            vmem((HALO, ROWS), BF),
            vmem((ROWS, ROWS + HALO), BF),
            vmem((ROWS, ROWS), BF),
            vmem((HALO, D), BF),
            vmem((ROWS, D), BF),
            vmem((ROWS, D), BF),
            vmem((3, ROWS, D), BF),
            vmem((ROWS, D), F32),
            vmem((ROWS, D), F32),
            vmem((ROWS, D), BF),
            vmem((ROWS, D), BF),
            vmem((D, D), F32),
            vmem((ROWS, D), BF),
            vmem((5, N_DOM, CAP, D), BF),
            vmem((5, N_DOM, CAP, D), BF),
            vmem((3, 32, 2, 8, D), BF),
            vmem((3, 32, 8, D), BF),
            vmem((N_GRP, 3, 32, 8, 128), BF),
            vmem((N_GRP - 1, 3, 32, 8, 128), BF),
            vmem((N_Y, 3, N_Z, 8, 128), BF),
            vmem((N_Y - 1, 3, N_Z, 8, 128), BF),
            vmem((N_Z, 3, 8, 128), BF),
            vmem((N_Z - 1, 3, 8, 128), BF),
            vmem((N_GRP, 3, 8, 128), F32),
            dma((7,)),
            dma((5,)),
            dma((5,)),
            dma((2, 3)),
            dma((2, 3, N_GRP - 1)),
            dma((2, N_Y - 1)),
            dma((2, N_Z - 1)),
            dma((2, N_GRP - 1)),
            dma((3,)),
        ],
        compiler_params=pltpu.CompilerParams(
            collective_id=0, has_side_effects=True, vmem_limit_bytes=56 << 20
        ),
        name="graph_step",
    )(blocks[0], wanted, features[0], history[:, 0], adj_tiles[0], weights, cotangent[0])
    return (embedding[None], fresh.reshape(2, 1, HALO, D), grads)


def solution(mesh):
    placed = (
        P("grp", "dom", None),
        P(None, "grp", "dom", None),
        P("grp", "dom", None, None, None),
        P("grp", "dom", None),
        P("grp", "dom", None, None),
        P("grp", "dom", None),
        P(),
        P("grp", "dom", None),
    )
    return jax.shard_map(
        body,
        mesh=mesh,
        in_specs=placed,
        out_specs=(P("grp", "dom", None), P(None, "grp", "dom", None), P(None, "dom", None)),
        check_vma=False,
    )
```

```python
import functools
import math

import jax
import jax.numpy as jnp
from jax import lax
from jax.experimental import pallas as pl
from jax.experimental.pallas import tpu as pltpu
from jax.sharding import PartitionSpec as P

MESH = pl.DeviceIdType.MESH
BF = jnp.bfloat16
F32 = jnp.float32
N_DOM, N_GRP, N_Z, N_Y = 64, 4, 8, 4
ROWS, D, HALO, CAP = 1024, 512, 512, 8
STEP = 256


def dot(a, b):
    return jnp.dot(a, b, preferred_element_type=F32)


def dot_rows(a, b):
    return lax.dot_general(a, b, (((0,), (0,)), ((), ())), preferred_element_type=F32)


def dot_t(a, b):
    return lax.dot_general(a, b, (((1,), (1,)), ((), ())), preferred_element_type=F32)


def step_kernel(
    blk, list_h, used_h, feat_h, hist_h, adj_h, w_h, cot_h,
    emb, fresh, wg_o,
    rows_of, used, feat, hist, adj, w, cot, hot, mix, back_mix, halo, h1, h2, mid, part, slope0, back2,
    dm, grad, acc, send, recv,
    wg, core_in, x_out, x_in, y_out, y_in, z_out, z_in, quarters,
    in_sem, send_sem, recv_sem, core_sem, x_sem, y_sem, z_sem, q_sem,
):
    me = lax.axis_index("dom")
    g = lax.axis_index("grp")
    z, y, c = me // 8, (me % 8) // 2, me % 2
    loads = [
        pltpu.make_async_copy(a, b, in_sem.at[i])
        for i, (a, b) in enumerate(
            [(list_h, rows_of), (used_h, used), (feat_h, feat), (hist_h.at[0], hist.at[0]), (hist_h.at[1], hist.at[1]),
             (adj_h, adj), (w_h, w), (cot_h, cot)]
        )
    ]
    for load in loads[:3]:
        load.start()

    barrier = pltpu.get_barrier_semaphore()

    def greet(s, _):
        pl.semaphore_signal(barrier, inc=1, device_id={"dom": lax.rem(me + s, N_DOM)}, device_id_type=MESH)
        return 0

    lax.fori_loop(1, N_DOM, greet, 0)
    for s in range(1, N_GRP):
        pl.semaphore_signal(barrier, inc=1, device_id={"grp": lax.rem(g + s, N_GRP)}, device_id_type=MESH)

    for load in loads[3:]:
        load.start()

    def slots(turn):
        return fresh.at[turn - 3] if turn >= 3 else recv.at[turn]

    def gather(rows_ref, turn):
        def one(i, _):
            rows = pl.ds(pl.multiple_of(i * STEP, STEP), STEP)
            picked = dot(hot[rows, :], rows_ref[...])
            send[turn, pl.ds(i * (STEP // CAP), STEP // CAP)] = picked.reshape(STEP // CAP, CAP, D).astype(BF)
            return 0

        lax.fori_loop(0, HALO // STEP, one, 0)

    def exchange(turn):
        def one(s, _):
            half = (s + 1) // 2
            to = jnp.where(lax.rem(s, 2) == 1, lax.rem(me + half, N_DOM), lax.rem(me + N_DOM - half, N_DOM))
            pltpu.make_async_remote_copy(
                send.at[turn, to], slots(turn).at[me], send_sem.at[turn], recv_sem.at[turn],
                device_id={"dom": to}, device_id_type=MESH,
            ).start()
            return 0

        lax.fori_loop(1, N_DOM, one, 0)

    def arrived(turn):
        block = slots(turn).at[pl.ds(0, N_DOM - 1)]
        pltpu.make_async_copy(block, block, recv_sem.at[turn]).wait()

    def unpack(turn):
        def one(i, _):
            part = recv[turn, pl.ds(i * 8, 8)].astype(F32).reshape(64, D)
            halo[pl.ds(pl.multiple_of(i * 64, 64), 64), :] = part.astype(BF)
            return 0

        lax.fori_loop(0, N_DOM // 8, one, 0)

    def own_part(rows_ref):
        def one(i, _):
            rows = pl.ds(pl.multiple_of(i * STEP, STEP), STEP)
            part[rows, :] = dot(mix[rows, 0:ROWS], rows_ref[...])
            return 0

        lax.fori_loop(0, ROWS // STEP, one, 0)

    def forward(layer, next_ref):
        def one(i, _):
            rows = pl.ds(pl.multiple_of(i * STEP, STEP), STEP)
            mixed = (part[rows, :] + dot(mix[rows, ROWS:ROWS + HALO], halo[...])).astype(BF)
            mid[layer, rows, :] = mixed
            value = dot(mixed, w[layer])
            if layer == 2:
                next_ref[rows, :] = value.astype(BF)
            else:
                gate = jax.nn.sigmoid(value)
                next_ref[rows, :] = (value * gate).astype(BF)
                slope = gate * (1.0 + value * (1.0 - gate))
                if layer == 0:
                    slope0[rows, :] = slope
                else:
                    grad[rows, :] = (back2[rows, :] * slope).astype(BF)
            return 0

        lax.fori_loop(0, ROWS // STEP, one, 0)

    def back_through(layer, grad_ref):
        def one(i, _):
            rows = pl.ds(pl.multiple_of(i * STEP, STEP), STEP)
            dm[rows, :] = dot_t(grad_ref[rows, :], w[layer]).astype(BF)
            return 0

        lax.fori_loop(0, ROWS // STEP, one, 0)

    def spread(last):
        def one(i, _):
            rows = pl.ds(pl.multiple_of(i * STEP, STEP), STEP)
            value = dot(back_mix[rows, :], dm[...])
            if last:
                grad[rows, :] = (value * slope0[rows, :]).astype(BF)
            else:
                back2[rows, :] = value
            return 0

        lax.fori_loop(0, ROWS // STEP, one, 0)

    def weight_grad(layer, grad_ref):
        acc[...] = jnp.zeros_like(acc)

        def one(i, _):
            rows = pl.ds(pl.multiple_of(i * STEP, STEP), STEP)
            acc[...] += dot_rows(mid[layer, rows, :], grad_ref[rows, :])
            return 0

        lax.fori_loop(0, ROWS // STEP, one, 0)
        wg[layer] = acc[...].reshape(32, 2, 8, D).astype(BF)
        core_copy(layer).start()

    def core_copy(layer):
        return pltpu.make_async_remote_copy(
            wg.at[layer, :, 1 - c], core_in.at[layer], core_sem.at[0, layer], core_sem.at[1, layer],
            device_id={"dom": me + 1 - 2 * c}, device_id_type=MESH,
        )

    def x_copy(layer, s):
        to = lax.rem(g + s, N_GRP)
        return pltpu.make_async_remote_copy(
            x_out.at[to, layer], x_in.at[s - 1, layer], x_sem.at[0, layer, s - 1], x_sem.at[1, layer, s - 1],
            device_id={"grp": to}, device_id_type=MESH,
        )

    def x_stage(layer):
        core_copy(layer).wait_recv()
        both = wg[layer, :, c].astype(F32) + core_in[layer].astype(F32)
        for q in range(N_GRP):
            x_out[q, layer] = both[:, :, q * 128:(q + 1) * 128].astype(BF)
        for s in range(1, N_GRP):
            x_copy(layer, s).start()

    def y_copy(layer, s):
        to = lax.rem(y + s, N_Y)
        return pltpu.make_async_remote_copy(
            y_out.at[to, layer], y_in.at[s - 1, layer], y_sem.at[0, layer, s - 1], y_sem.at[1, layer, s - 1],
            device_id={"dom": z * 8 + to * 2 + c}, device_id_type=MESH,
        )

    def z_copy(s):
        to = lax.rem(z + s, N_Z)
        return pltpu.make_async_remote_copy(
            z_out.at[to], z_in.at[s - 1], z_sem.at[0, s - 1], z_sem.at[1, s - 1],
            device_id={"dom": to * 8 + y * 2 + c}, device_id_type=MESH,
        )

    def q_copy(s):
        return pltpu.make_async_remote_copy(
            quarters.at[g], quarters.at[g], q_sem.at[0, s - 1], q_sem.at[1, s - 1],
            device_id={"grp": lax.rem(g + s, N_GRP)}, device_id_type=MESH,
        )

    def y_stage(layer):
        for s in range(1, N_GRP):
            x_copy(layer, s).wait_recv()
        total = x_out[g, layer].astype(F32)
        for s in range(1, N_GRP):
            total = total + x_in[s - 1, layer].astype(F32)
        total = total.reshape(N_Z, N_Y, 8, 128)
        for to in range(N_Y):
            y_out[to, layer] = total[:, to].astype(BF)
        for s in range(1, N_Y):
            y_copy(layer, s).start()

    def z_prepare(layer):
        for s in range(1, N_Y):
            y_copy(layer, s).wait_recv()
        total = y_out[y, layer].astype(F32)
        for s in range(1, N_Y):
            total = total + y_in[s - 1, layer].astype(F32)
        for to in range(N_Z):
            z_out[to, layer] = total[to].astype(BF)

    loads[0].wait()
    loads[1].wait()
    slot = lax.broadcasted_iota(jnp.int32, (CAP, N_DOM), 0)
    wanted = jnp.where(slot < used[...], rows_of[...], -1)
    lane = lax.broadcasted_iota(jnp.int32, (2 * CAP, 128), 1)
    for p in range(0, N_DOM, 2):
        pair = jnp.concatenate(
            [jnp.broadcast_to(wanted[:, q:q + 1], (CAP, 128)) for q in (p, p + 1)], axis=0
        )
        for k in range(ROWS // 128):
            hot[p * CAP:(p + 2) * CAP, k * 128:(k + 1) * 128] = jnp.where(pair == lane + k * 128, 1.0, 0.0).astype(BF)
    loads[2].wait()
    gather(feat, 0)
    for turn in range(5):
        slots(turn)[me] = jnp.zeros((CAP, D), BF)
    pl.semaphore_wait(barrier, N_DOM - 1 + N_GRP - 1)
    exchange(0)
    loads[3].wait()
    gather(hist.at[0], 1)
    exchange(1)
    loads[4].wait()
    gather(hist.at[1], 2)
    exchange(2)

    loads[5].wait()
    for b in range(8):
        tiles = [adj[b, k].astype(F32) for k in range(4)]
        rows = slice(b * 128, (b + 1) * 128)
        for j in range(12):
            if j < 8:
                entry = jnp.where(blk[1, b] == j, tiles[1], 0.0)
                if j == b:
                    entry = entry + tiles[0]
            else:
                entry = jnp.where(blk[1, b] == j, tiles[1], 0.0)
                entry = entry + jnp.where(blk[2, b] == j, tiles[2], 0.0)
                entry = entry + jnp.where(blk[3, b] == j, tiles[3], 0.0)
            mix[rows, j * 128:(j + 1) * 128] = entry.astype(BF)
            if j < 8:
                back_mix[j * 128:(j + 1) * 128, rows] = entry.T.astype(BF)

    loads[6].wait()
    loads[7].wait()
    own_part(feat)
    back_through(2, cot)
    spread(False)

    arrived(0)
    unpack(0)
    forward(0, h1)
    gather(h1, 3)
    exchange(3)
    own_part(h1)

    arrived(1)
    unpack(1)
    forward(1, h2)
    gather(h2, 4)
    exchange(4)

    weight_grad(1, grad)
    back_through(1, grad)
    spread(True)
    x_stage(1)
    weight_grad(0, grad)
    own_part(h2)
    x_stage(0)

    arrived(2)
    unpack(2)
    forward(2, emb)
    weight_grad(2, cot)
    y_stage(1)
    x_stage(2)
    y_stage(0)
    z_prepare(1)
    y_stage(2)
    z_prepare(0)
    z_prepare(2)
    for s in range(1, N_Z):
        z_copy(s).start()
    for s in range(1, N_Z):
        z_copy(s).wait_recv()
    total = z_out[z].astype(F32)
    for s in range(1, N_Z):
        total = total + z_in[s - 1].astype(F32)
    quarters[g] = total * (1.0 / math.sqrt(N_GRP * N_DOM * ROWS))
    for s in range(1, N_GRP):
        q_copy(s).start()

    for s in range(1, N_GRP):
        q_copy(s).wait_recv()
    for q in range(N_GRP):
        wg_o[:, :, q * 128:(q + 1) * 128] = quarters[q]

    arrived(3)
    arrived(4)
    for turn in range(5):
        block = send.at[turn, pl.ds(0, N_DOM - 1)]
        pltpu.make_async_copy(block, block, send_sem.at[turn]).wait()
    for layer in range(3):
        core_copy(layer).wait_send()
        for s in range(1, N_GRP):
            x_copy(layer, s).wait_send()
        for s in range(1, N_Y):
            y_copy(layer, s).wait_send()
    for s in range(1, N_Z):
        z_copy(s).wait_send()
    for s in range(1, N_GRP):
        q_copy(s).wait_send()


def out_kernel(emb, fresh, grads, emb_o, fresh_o, grads_o, sem):
    copies = [
        pltpu.make_async_copy(a, b, sem.at[i])
        for i, (a, b) in enumerate([(emb, emb_o), (fresh, fresh_o), (grads, grads_o)])
    ]
    for copy in copies:
        copy.start()
    for copy in copies:
        copy.wait()


def body(features, history, adj_tiles, blocks, send_list, counts, weights, cotangent):
    vmem = pltpu.VMEM
    dma = pltpu.SemaphoreType.DMA
    whole = pl.BlockSpec(memory_space=vmem)
    anywhere = pl.BlockSpec(memory_space=pl.ANY)
    shapes = (((ROWS, D), BF), ((2, N_DOM, CAP, D), BF), ((3, 8, D), F32))
    made = pl.pallas_call(
        step_kernel,
        out_shape=tuple(vmem(*shape) for shape in shapes),
        in_specs=[pl.BlockSpec(memory_space=pltpu.SMEM)] + [anywhere] * 7,
        out_specs=(whole,) * 3,
        scratch_shapes=[
            vmem((CAP, N_DOM), jnp.int32),
            vmem((1, N_DOM), jnp.int32),
            vmem((ROWS, D), BF),
            vmem((2, ROWS, D), BF),
            vmem((8, 4, 128, 128), BF),
            vmem((3, D, D), BF),
            vmem((ROWS, D), BF),
            vmem((HALO, ROWS), BF),
            vmem((ROWS, ROWS + HALO), BF),
            vmem((ROWS, ROWS), BF),
            vmem((HALO, D), BF),
            vmem((ROWS, D), BF),
            vmem((ROWS, D), BF),
            vmem((3, ROWS, D), BF),
            vmem((ROWS, D), F32),
            vmem((ROWS, D), F32),
            vmem((ROWS, D), F32),
            vmem((ROWS, D), BF),
            vmem((ROWS, D), BF),
            vmem((D, D), F32),
            vmem((5, N_DOM, CAP, D), BF),
            vmem((3, N_DOM, CAP, D), BF),
            vmem((3, 32, 2, 8, D), BF),
            vmem((3, 32, 8, D), BF),
            vmem((N_GRP, 3, 32, 8, 128), BF),
            vmem((N_GRP - 1, 3, 32, 8, 128), BF),
            vmem((N_Y, 3, N_Z, 8, 128), BF),
            vmem((N_Y - 1, 3, N_Z, 8, 128), BF),
            vmem((N_Z, 3, 8, 128), BF),
            vmem((N_Z - 1, 3, 8, 128), BF),
            vmem((N_GRP, 3, 8, 128), F32),
            dma((8,)),
            dma((5,)),
            dma((5,)),
            dma((2, 3)),
            dma((2, 3, N_GRP - 1)),
            dma((2, 3, N_Y - 1)),
            dma((2, N_Z - 1)),
            dma((2, N_GRP - 1)),
        ],
        compiler_params=pltpu.CompilerParams(
            collective_id=0, has_side_effects=True, vmem_limit_bytes=56 << 20
        ),
        name="graph_step",
    )(
        blocks[0].T, send_list[0, 0].T, counts[0], features[0], history[:, 0], adj_tiles[0], weights, cotangent[0]
    )
    made = [pltpu.with_memory_space_constraint(piece, pltpu.VMEM) for piece in made]
    embedding, fresh, grads = pl.pallas_call(
        out_kernel,
        out_shape=tuple(jax.ShapeDtypeStruct(*shape) for shape in shapes),
        in_specs=[whole] * 3,
        out_specs=(anywhere,) * 3,
        scratch_shapes=[dma((3,))],
        name="outputs",
    )(*made)
    return (embedding[None], fresh.reshape(2, 1, HALO, D), grads)


def solution(mesh):
    placed = (
        P("grp", "dom", None),
        P(None, "grp", "dom", None),
        P("grp", "dom", None, None, None),
        P("grp", "dom", None),
        P("grp", "dom", None, None),
        P("grp", "dom", None),
        P(),
        P("grp", "dom", None),
    )
    return jax.shard_map(
        body,
        mesh=mesh,
        in_specs=placed,
        out_specs=(P("grp", "dom", None), P(None, "grp", "dom", None), P(None, "dom", None)),
        check_vma=False,
    )
```

```python
import functools
import math

import jax
import jax.numpy as jnp
from jax import lax
from jax.experimental import pallas as pl
from jax.experimental.pallas import tpu as pltpu
from jax.sharding import PartitionSpec as P

MESH = pl.DeviceIdType.MESH
BF = jnp.bfloat16
F32 = jnp.float32
N_DOM, N_GRP, N_Z, N_Y = 64, 4, 8, 4
ROWS, D, HALO, CAP = 1024, 512, 512, 8
STEP = 1024
HELD = 32


def dot(a, b):
    return jnp.dot(a, b, preferred_element_type=F32)


def dot_rows(a, b):
    return lax.dot_general(a, b, (((0,), (0,)), ((), ())), preferred_element_type=F32)


def dot_t(a, b):
    return lax.dot_general(a, b, (((1,), (1,)), ((), ())), preferred_element_type=F32)


def step_kernel(
    blk, list_h, used_h, feat_h, hist_h, adj_h, w_h, cot_h,
    emb, fresh, wg_o,
    rows_of, used, feat, hist, adj, w, cot, hot, mix, back_mix, halo, h1, h2, mid, part, slope0, back2,
    dm, grad, acc, send, recv,
    wg, core_in, x_out, x_in, y_out, y_in, z_out, z_in, quarters,
    in_sem, send_sem, recv_sem, core_sem, x_sem, y_sem, z_sem, q_sem,
):
    me = lax.axis_index("dom")
    g = lax.axis_index("grp")
    z, y, c = me // 8, (me % 8) // 2, me % 2
    loads = [
        pltpu.make_async_copy(a, b, in_sem.at[i])
        for i, (a, b) in enumerate(
            [(list_h, rows_of), (used_h, used), (feat_h, feat), (hist_h.at[0], hist.at[0]), (hist_h.at[1], hist.at[1]),
             (adj_h, adj), (w_h, w), (cot_h, cot)]
        )
    ]
    for load in loads[:3]:
        load.start()

    barrier = pltpu.get_barrier_semaphore()

    def greet(s, _):
        pl.semaphore_signal(barrier, inc=1, device_id={"dom": lax.rem(me + s, N_DOM)}, device_id_type=MESH)
        return 0

    lax.fori_loop(1, N_DOM, greet, 0)
    for s in range(1, N_GRP):
        pl.semaphore_signal(barrier, inc=1, device_id={"grp": lax.rem(g + s, N_GRP)}, device_id_type=MESH)

    for load in loads[3:]:
        load.start()

    def slots(turn):
        return fresh.at[turn - 3] if turn >= 3 else recv.at[turn]

    def gather(rows_ref, turn):
        def one(i, _):
            rows = pl.ds(pl.multiple_of(i * HALO, HALO), HALO)
            picked = dot(hot[rows, :], rows_ref[...])
            send[turn, pl.ds(i * (HALO // CAP), HALO // CAP)] = picked.reshape(HALO // CAP, CAP, D).astype(BF)
            return 0

        lax.fori_loop(0, 1, one, 0)

    def exchange(turn, first=1, last=N_DOM):
        def one(i, _):
            s = N_DOM - i if turn == 4 else i
            half = (s + 1) // 2
            to = jnp.where(lax.rem(s, 2) == 1, lax.rem(me + half, N_DOM), lax.rem(me + N_DOM - half, N_DOM))
            pltpu.make_async_remote_copy(
                send.at[turn, to], slots(turn).at[me], send_sem.at[turn], recv_sem.at[turn],
                device_id={"dom": to}, device_id_type=MESH,
            ).start()
            return 0

        lax.fori_loop(first, last, one, 0)

    def arrived(turn):
        block = slots(turn).at[pl.ds(0, N_DOM - 1)]
        pltpu.make_async_copy(block, block, recv_sem.at[turn]).wait()

    def unpack(turn):
        def one(i, _):
            part = recv[turn, pl.ds(i * 8, 8)].astype(F32).reshape(64, D)
            halo[pl.ds(pl.multiple_of(i * 64, 64), 64), :] = part.astype(BF)
            return 0

        lax.fori_loop(0, N_DOM // 8, one, 0)

    def own_part(rows_ref):
        def one(i, _):
            rows = pl.ds(pl.multiple_of(i * STEP, STEP), STEP)
            part[rows, :] = dot(mix[rows, 0:ROWS], rows_ref[...])
            return 0

        lax.fori_loop(0, ROWS // STEP, one, 0)

    def forward(layer, next_ref):
        def one(i, _):
            rows = pl.ds(pl.multiple_of(i * STEP, STEP), STEP)
            mixed = (part[rows, :] + dot(mix[rows, ROWS:ROWS + HALO], halo[...])).astype(BF)
            mid[layer, rows, :] = mixed
            value = dot(mixed, w[layer])
            if layer == 2:
                next_ref[rows, :] = value.astype(BF)
            else:
                gate = jax.nn.sigmoid(value)
                next_ref[rows, :] = (value * gate).astype(BF)
                slope = gate * (1.0 + value * (1.0 - gate))
                if layer == 0:
                    slope0[rows, :] = slope
                else:
                    grad[rows, :] = (back2[rows, :] * slope).astype(BF)
            return 0

        lax.fori_loop(0, ROWS // STEP, one, 0)

    def back_through(layer, grad_ref):
        def one(i, _):
            rows = pl.ds(pl.multiple_of(i * STEP, STEP), STEP)
            dm[rows, :] = dot_t(grad_ref[rows, :], w[layer]).astype(BF)
            return 0

        lax.fori_loop(0, ROWS // STEP, one, 0)

    def spread(last):
        def one(i, _):
            rows = pl.ds(pl.multiple_of(i * STEP, STEP), STEP)
            value = dot(back_mix[rows, :], dm[...])
            if last:
                grad[rows, :] = (value * slope0[rows, :]).astype(BF)
            else:
                back2[rows, :] = value
            return 0

        lax.fori_loop(0, ROWS // STEP, one, 0)

    def weight_grad(layer, grad_ref):
        acc[...] = jnp.zeros_like(acc)

        def one(i, _):
            rows = pl.ds(pl.multiple_of(i * STEP, STEP), STEP)
            acc[...] += dot_rows(mid[layer, rows, :], grad_ref[rows, :])
            return 0

        lax.fori_loop(0, ROWS // STEP, one, 0)
        wg[layer] = acc[...].reshape(32, 2, 8, D).astype(BF)
        core_copy(layer).start()

    def core_copy(layer):
        return pltpu.make_async_remote_copy(
            wg.at[layer, :, 1 - c], core_in.at[layer], core_sem.at[0, layer], core_sem.at[1, layer],
            device_id={"dom": me + 1 - 2 * c}, device_id_type=MESH,
        )

    def x_copy(layer, s):
        to = lax.rem(g + s, N_GRP)
        return pltpu.make_async_remote_copy(
            x_out.at[to, layer], x_in.at[s - 1, layer], x_sem.at[0, layer, s - 1], x_sem.at[1, layer, s - 1],
            device_id={"grp": to}, device_id_type=MESH,
        )

    def x_stage(layer):
        core_copy(layer).wait_recv()
        both = wg[layer, :, c].astype(F32) + core_in[layer].astype(F32)
        for q in range(N_GRP):
            x_out[q, layer] = both[:, :, q * 128:(q + 1) * 128].astype(BF)
        for s in range(1, N_GRP):
            x_copy(layer, s).start()

    def y_copy(layer, s):
        to = lax.rem(y + s, N_Y)
        return pltpu.make_async_remote_copy(
            y_out.at[to, layer], y_in.at[s - 1, layer], y_sem.at[0, layer, s - 1], y_sem.at[1, layer, s - 1],
            device_id={"dom": z * 8 + to * 2 + c}, device_id_type=MESH,
        )

    def z_copy(s):
        to = lax.rem(z + s, N_Z)
        return pltpu.make_async_remote_copy(
            z_out.at[to], z_in.at[s - 1], z_sem.at[0, s - 1], z_sem.at[1, s - 1],
            device_id={"dom": to * 8 + y * 2 + c}, device_id_type=MESH,
        )

    def q_copy(s):
        return pltpu.make_async_remote_copy(
            quarters.at[g], quarters.at[g], q_sem.at[0, s - 1], q_sem.at[1, s - 1],
            device_id={"grp": lax.rem(g + s, N_GRP)}, device_id_type=MESH,
        )

    def y_stage(layer):
        for s in range(1, N_GRP):
            x_copy(layer, s).wait_recv()
        total = x_out[g, layer].astype(F32)
        for s in range(1, N_GRP):
            total = total + x_in[s - 1, layer].astype(F32)
        total = total.reshape(N_Z, N_Y, 8, 128)
        for to in range(N_Y):
            y_out[to, layer] = total[:, to].astype(BF)
        for s in range(1, N_Y):
            y_copy(layer, s).start()

    def z_prepare(layer):
        for s in range(1, N_Y):
            y_copy(layer, s).wait_recv()
        total = y_out[y, layer].astype(F32)
        for s in range(1, N_Y):
            total = total + y_in[s - 1, layer].astype(F32)
        for to in range(N_Z):
            z_out[to, layer] = total[to].astype(BF)

    loads[0].wait()
    loads[1].wait()
    slot = lax.broadcasted_iota(jnp.int32, (CAP, N_DOM), 0)
    wanted = jnp.where(slot < used[...], rows_of[...], -1)
    lane = lax.broadcasted_iota(jnp.int32, (2 * CAP, 128), 1)
    for p in range(0, N_DOM, 2):
        pair = jnp.concatenate(
            [jnp.broadcast_to(wanted[:, q:q + 1], (CAP, 128)) for q in (p, p + 1)], axis=0
        )
        for k in range(ROWS // 128):
            hot[p * CAP:(p + 2) * CAP, k * 128:(k + 1) * 128] = jnp.where(pair == lane + k * 128, 1.0, 0.0).astype(BF)
    loads[2].wait()
    gather(feat, 0)
    for turn in range(5):
        slots(turn)[me] = jnp.zeros((CAP, D), BF)
    pl.semaphore_wait(barrier, N_DOM - 1 + N_GRP - 1)
    exchange(0)
    loads[3].wait()
    gather(hist.at[0], 1)
    exchange(1)
    loads[4].wait()
    gather(hist.at[1], 2)
    exchange(2)

    loads[5].wait()
    for b in range(8):
        tiles = [adj[b, k].astype(F32) for k in range(4)]
        rows = slice(b * 128, (b + 1) * 128)
        for j in range(12):
            if j < 8:
                entry = jnp.where(blk[1, b] == j, tiles[1], 0.0)
                if j == b:
                    entry = entry + tiles[0]
            else:
                entry = jnp.where(blk[1, b] == j, tiles[1], 0.0)
                entry = entry + jnp.where(blk[2, b] == j, tiles[2], 0.0)
                entry = entry + jnp.where(blk[3, b] == j, tiles[3], 0.0)
            mix[rows, j * 128:(j + 1) * 128] = entry.astype(BF)
            if j < 8:
                back_mix[j * 128:(j + 1) * 128, rows] = entry.T.astype(BF)

    loads[6].wait()
    loads[7].wait()
    own_part(feat)
    back_through(2, cot)
    spread(False)

    arrived(0)
    unpack(0)
    forward(0, h1)
    gather(h1, 3)
    exchange(3)
    own_part(h1)

    arrived(1)
    unpack(1)
    forward(1, h2)
    gather(h2, 4)
    exchange(4, 1, HELD)

    weight_grad(1, grad)
    back_through(1, grad)
    spread(True)
    x_stage(1)
    weight_grad(0, grad)
    own_part(h2)
    x_stage(0)

    arrived(2)
    unpack(2)
    forward(2, emb)
    weight_grad(2, cot)
    y_stage(1)
    x_stage(2)
    y_stage(0)
    z_prepare(1)
    y_stage(2)
    z_prepare(0)
    z_prepare(2)
    for s in range(1, N_Z):
        z_copy(s).start()
    exchange(4, HELD, N_DOM)
    for s in range(1, N_Z):
        z_copy(s).wait_recv()
    total = z_out[z].astype(F32)
    for s in range(1, N_Z):
        total = total + z_in[s - 1].astype(F32)
    quarters[g] = total * (1.0 / math.sqrt(N_GRP * N_DOM * ROWS))
    for s in range(1, N_GRP):
        q_copy(s).start()

    for s in range(1, N_GRP):
        q_copy(s).wait_recv()
    for q in range(N_GRP):
        wg_o[:, :, q * 128:(q + 1) * 128] = quarters[q]

    arrived(3)
    arrived(4)
    for turn in range(5):
        block = send.at[turn, pl.ds(0, N_DOM - 1)]
        pltpu.make_async_copy(block, block, send_sem.at[turn]).wait()
    for layer in range(3):
        core_copy(layer).wait_send()
        for s in range(1, N_GRP):
            x_copy(layer, s).wait_send()
        for s in range(1, N_Y):
            y_copy(layer, s).wait_send()
    for s in range(1, N_Z):
        z_copy(s).wait_send()
    for s in range(1, N_GRP):
        q_copy(s).wait_send()


def out_kernel(emb, fresh, grads, emb_o, fresh_o, grads_o, sem):
    copies = [
        pltpu.make_async_copy(a, b, sem.at[i])
        for i, (a, b) in enumerate([(emb, emb_o), (fresh, fresh_o), (grads, grads_o)])
    ]
    for copy in copies:
        copy.start()
    for copy in copies:
        copy.wait()


def body(features, history, adj_tiles, blocks, send_list, counts, weights, cotangent):
    vmem = pltpu.VMEM
    dma = pltpu.SemaphoreType.DMA
    whole = pl.BlockSpec(memory_space=vmem)
    anywhere = pl.BlockSpec(memory_space=pl.ANY)
    shapes = (((ROWS, D), BF), ((2, N_DOM, CAP, D), BF), ((3, 8, D), F32))
    made = pl.pallas_call(
        step_kernel,
        out_shape=tuple(vmem(*shape) for shape in shapes),
        in_specs=[pl.BlockSpec(memory_space=pltpu.SMEM)] + [anywhere] * 7,
        out_specs=(whole,) * 3,
        scratch_shapes=[
            vmem((CAP, N_DOM), jnp.int32),
            vmem((1, N_DOM), jnp.int32),
            vmem((ROWS, D), BF),
            vmem((2, ROWS, D), BF),
            vmem((8, 4, 128, 128), BF),
            vmem((3, D, D), BF),
            vmem((ROWS, D), BF),
            vmem((HALO, ROWS), BF),
            vmem((ROWS, ROWS + HALO), BF),
            vmem((ROWS, ROWS), BF),
            vmem((HALO, D), BF),
            vmem((ROWS, D), BF),
            vmem((ROWS, D), BF),
            vmem((3, ROWS, D), BF),
            vmem((ROWS, D), F32),
            vmem((ROWS, D), F32),
            vmem((ROWS, D), F32),
            vmem((ROWS, D), BF),
            vmem((ROWS, D), BF),
            vmem((D, D), F32),
            vmem((5, N_DOM, CAP, D), BF),
            vmem((3, N_DOM, CAP, D), BF),
            vmem((3, 32, 2, 8, D), BF),
            vmem((3, 32, 8, D), BF),
            vmem((N_GRP, 3, 32, 8, 128), BF),
            vmem((N_GRP - 1, 3, 32, 8, 128), BF),
            vmem((N_Y, 3, N_Z, 8, 128), BF),
            vmem((N_Y - 1, 3, N_Z, 8, 128), BF),
            vmem((N_Z, 3, 8, 128), BF),
            vmem((N_Z - 1, 3, 8, 128), BF),
            vmem((N_GRP, 3, 8, 128), F32),
            dma((8,)),
            dma((5,)),
            dma((5,)),
            dma((2, 3)),
            dma((2, 3, N_GRP - 1)),
            dma((2, 3, N_Y - 1)),
            dma((2, N_Z - 1)),
            dma((2, N_GRP - 1)),
        ],
        compiler_params=pltpu.CompilerParams(
            collective_id=0, has_side_effects=True, vmem_limit_bytes=56 << 20
        ),
        name="graph_step",
    )(
        blocks[0].T, send_list[0, 0].T, counts[0], features[0], history[:, 0], adj_tiles[0], weights, cotangent[0]
    )
    made = [pltpu.with_memory_space_constraint(piece, pltpu.VMEM) for piece in made]
    embedding, fresh, grads = pl.pallas_call(
        out_kernel,
        out_shape=tuple(jax.ShapeDtypeStruct(*shape) for shape in shapes),
        in_specs=[whole] * 3,
        out_specs=(anywhere,) * 3,
        scratch_shapes=[dma((3,))],
        name="outputs",
    )(*made)
    return (embedding[None], fresh.reshape(2, 1, HALO, D), grads)


def solution(mesh):
    placed = (
        P("grp", "dom", None),
        P(None, "grp", "dom", None),
        P("grp", "dom", None, None, None),
        P("grp", "dom", None),
        P("grp", "dom", None, None),
        P("grp", "dom", None),
        P(),
        P("grp", "dom", None),
    )
    return jax.shard_map(
        body,
        mesh=mesh,
        in_specs=placed,
        out_specs=(P("grp", "dom", None), P(None, "grp", "dom", None), P(None, "dom", None)),
        check_vma=False,
    )
```

```python
import functools
import math

import jax
import jax.numpy as jnp
from jax import lax
from jax.experimental import pallas as pl
from jax.experimental.pallas import tpu as pltpu
from jax.sharding import PartitionSpec as P

MESH = pl.DeviceIdType.MESH
BF = jnp.bfloat16
F32 = jnp.float32
N_DOM, N_GRP, N_Z, N_Y = 64, 4, 8, 4
ROWS, D, HALO, CAP = 1024, 512, 512, 8
STEP = 1024
HELD = 32


def dot(a, b):
    return jnp.dot(a, b, preferred_element_type=F32)


def dot_rows(a, b):
    return lax.dot_general(a, b, (((0,), (0,)), ((), ())), preferred_element_type=F32)


def dot_t(a, b):
    return lax.dot_general(a, b, (((1,), (1,)), ((), ())), preferred_element_type=F32)


def step_kernel(
    blk, list_h, used_h, feat_h, hist_h, adj_h, w_h, cot_h,
    emb, fresh, wg_o,
    rows_of, used, feat, hist, adj, w, cot, hot, mix, back_mix, halo, h1, h2, mid, part, slope0, back2,
    dm, grad, send, recv,
    wg, core_in, x_out, x_in, y_out, y_in, z_out, z_in, quarters,
    in_sem, send_sem, recv_sem, core_sem, x_sem, y_sem, z_sem, q_sem,
):
    me = lax.axis_index("dom")
    g = lax.axis_index("grp")
    z, y, c = me // 8, (me % 8) // 2, me % 2
    loads = [
        pltpu.make_async_copy(a, b, in_sem.at[i])
        for i, (a, b) in enumerate(
            [(list_h, rows_of), (used_h, used), (feat_h, feat), (hist_h.at[0], hist.at[0]), (hist_h.at[1], hist.at[1]),
             (adj_h, adj), (w_h, w), (cot_h, cot)]
        )
    ]
    for load in loads[:3]:
        load.start()

    barrier = pltpu.get_barrier_semaphore()

    def greet(s, _):
        pl.semaphore_signal(barrier, inc=1, device_id={"dom": lax.rem(me + s, N_DOM)}, device_id_type=MESH)
        return 0

    lax.fori_loop(1, N_DOM, greet, 0)
    for s in range(1, N_GRP):
        pl.semaphore_signal(barrier, inc=1, device_id={"grp": lax.rem(g + s, N_GRP)}, device_id_type=MESH)

    for load in loads[3:]:
        load.start()

    def slots(turn):
        return fresh.at[turn - 3] if turn >= 3 else recv.at[turn]

    def gather(rows_ref, turn):
        def one(i, _):
            rows = pl.ds(pl.multiple_of(i * HALO, HALO), HALO)
            picked = dot(hot[rows, :], rows_ref[...])
            send[turn, pl.ds(i * (HALO // CAP), HALO // CAP)] = picked.reshape(HALO // CAP, CAP, D).astype(BF)
            return 0

        lax.fori_loop(0, 1, one, 0)

    def exchange(turn, first=1, last=N_DOM):
        def one(i, _):
            s = N_DOM - i
            half = (s + 1) // 2
            to = jnp.where(lax.rem(s, 2) == 1, lax.rem(me + half, N_DOM), lax.rem(me + N_DOM - half, N_DOM))
            pltpu.make_async_remote_copy(
                send.at[turn, to], slots(turn).at[me], send_sem.at[turn], recv_sem.at[turn],
                device_id={"dom": to}, device_id_type=MESH,
            ).start()
            return 0

        lax.fori_loop(first, last, one, 0)

    def arrived(turn):
        block = slots(turn).at[pl.ds(0, N_DOM - 1)]
        pltpu.make_async_copy(block, block, recv_sem.at[turn]).wait()

    def unpack(turn):
        def one(i, _):
            part = recv[turn, pl.ds(i * 8, 8)].astype(F32).reshape(64, D)
            halo[pl.ds(pl.multiple_of(i * 64, 64), 64), :] = part.astype(BF)
            return 0

        lax.fori_loop(0, N_DOM // 8, one, 0)

    def own_part(rows_ref):
        def one(i, _):
            rows = pl.ds(pl.multiple_of(i * STEP, STEP), STEP)
            part[rows, :] = dot(mix[rows, 0:ROWS], rows_ref[...])
            return 0

        lax.fori_loop(0, ROWS // STEP, one, 0)

    def forward(layer, next_ref):
        def one(i, _):
            rows = pl.ds(pl.multiple_of(i * STEP, STEP), STEP)
            mixed = (part[rows, :] + dot(mix[rows, ROWS:ROWS + HALO], halo[...])).astype(BF)
            mid[layer, rows, :] = mixed
            value = dot(mixed, w[layer])
            if layer == 2:
                next_ref[rows, :] = value.astype(BF)
            else:
                gate = jax.nn.sigmoid(value)
                next_ref[rows, :] = (value * gate).astype(BF)
                slope = gate * (1.0 + value * (1.0 - gate))
                if layer == 0:
                    slope0[rows, :] = slope
                else:
                    grad[rows, :] = (back2[rows, :] * slope).astype(BF)
            return 0

        lax.fori_loop(0, ROWS // STEP, one, 0)

    def back_through(layer, grad_ref):
        def one(i, _):
            rows = pl.ds(pl.multiple_of(i * STEP, STEP), STEP)
            dm[rows, :] = dot_t(grad_ref[rows, :], w[layer]).astype(BF)
            return 0

        lax.fori_loop(0, ROWS // STEP, one, 0)

    def spread(last):
        def one(i, _):
            rows = pl.ds(pl.multiple_of(i * STEP, STEP), STEP)
            value = dot(back_mix[rows, :], dm[...])
            if last:
                grad[rows, :] = (value * slope0[rows, :]).astype(BF)
            else:
                back2[rows, :] = value
            return 0

        lax.fori_loop(0, ROWS // STEP, one, 0)

    def weight_grad(layer, grad_ref):
        wg[layer] = dot_rows(mid[layer], grad_ref[...]).reshape(32, 2, 8, D).astype(BF)
        core_copy(layer).start()

    def core_copy(layer):
        return pltpu.make_async_remote_copy(
            wg.at[layer, :, 1 - c], core_in.at[layer], core_sem.at[0, layer], core_sem.at[1, layer],
            device_id={"dom": me + 1 - 2 * c}, device_id_type=MESH,
        )

    def x_copy(layer, s):
        to = lax.rem(g + s, N_GRP)
        return pltpu.make_async_remote_copy(
            x_out.at[to, layer], x_in.at[s - 1, layer], x_sem.at[0, layer, s - 1], x_sem.at[1, layer, s - 1],
            device_id={"grp": to}, device_id_type=MESH,
        )

    def x_stage(layer):
        core_copy(layer).wait_recv()
        both = wg[layer, :, c].astype(F32) + core_in[layer].astype(F32)
        for q in range(N_GRP):
            x_out[q, layer] = both[:, :, q * 128:(q + 1) * 128].astype(BF)
        for s in range(1, N_GRP):
            x_copy(layer, s).start()

    def y_copy(layer, s):
        to = lax.rem(y + s, N_Y)
        return pltpu.make_async_remote_copy(
            y_out.at[to, layer], y_in.at[s - 1, layer], y_sem.at[0, layer, s - 1], y_sem.at[1, layer, s - 1],
            device_id={"dom": z * 8 + to * 2 + c}, device_id_type=MESH,
        )

    def z_copy(s):
        to = lax.rem(z + s, N_Z)
        return pltpu.make_async_remote_copy(
            z_out.at[to], z_in.at[s - 1], z_sem.at[0, s - 1], z_sem.at[1, s - 1],
            device_id={"dom": to * 8 + y * 2 + c}, device_id_type=MESH,
        )

    def q_copy(s):
        return pltpu.make_async_remote_copy(
            quarters.at[g], quarters.at[g], q_sem.at[0, s - 1], q_sem.at[1, s - 1],
            device_id={"grp": lax.rem(g + s, N_GRP)}, device_id_type=MESH,
        )

    def y_stage(layer):
        for s in range(1, N_GRP):
            x_copy(layer, s).wait_recv()
        total = x_out[g, layer].astype(F32)
        for s in range(1, N_GRP):
            total = total + x_in[s - 1, layer].astype(F32)
        total = total.reshape(N_Z, N_Y, 8, 128)
        for to in range(N_Y):
            y_out[to, layer] = total[:, to].astype(BF)
        for s in range(1, N_Y):
            y_copy(layer, s).start()

    def z_prepare(layer):
        for s in range(1, N_Y):
            y_copy(layer, s).wait_recv()
        total = y_out[y, layer].astype(F32)
        for s in range(1, N_Y):
            total = total + y_in[s - 1, layer].astype(F32)
        for to in range(N_Z):
            z_out[to, layer] = total[to].astype(BF)

    loads[0].wait()
    loads[1].wait()
    slot = lax.broadcasted_iota(jnp.int32, (CAP, N_DOM), 0)
    wanted = jnp.where(slot < used[...], rows_of[...], -1)
    lane = lax.broadcasted_iota(jnp.int32, (2 * CAP, 128), 1)
    for p in range(0, N_DOM, 2):
        pair = jnp.concatenate(
            [jnp.broadcast_to(wanted[:, q:q + 1], (CAP, 128)) for q in (p, p + 1)], axis=0
        )
        for k in range(ROWS // 128):
            hot[p * CAP:(p + 2) * CAP, k * 128:(k + 1) * 128] = jnp.where(pair == lane + k * 128, 1.0, 0.0).astype(BF)
    loads[2].wait()
    gather(feat, 0)
    for turn in range(5):
        slots(turn)[me] = jnp.zeros((CAP, D), BF)
    pl.semaphore_wait(barrier, N_DOM - 1 + N_GRP - 1)
    exchange(0)
    loads[3].wait()
    gather(hist.at[0], 1)
    exchange(1)
    loads[4].wait()
    gather(hist.at[1], 2)
    exchange(2)

    loads[5].wait()
    for b in range(8):
        tiles = [adj[b, k].astype(F32) for k in range(4)]
        rows = slice(b * 128, (b + 1) * 128)
        for j in range(12):
            if j < 8:
                entry = jnp.where(blk[1, b] == j, tiles[1], 0.0)
                if j == b:
                    entry = entry + tiles[0]
            else:
                entry = jnp.where(blk[1, b] == j, tiles[1], 0.0)
                entry = entry + jnp.where(blk[2, b] == j, tiles[2], 0.0)
                entry = entry + jnp.where(blk[3, b] == j, tiles[3], 0.0)
            mix[rows, j * 128:(j + 1) * 128] = entry.astype(BF)
            if j < 8:
                back_mix[j * 128:(j + 1) * 128, rows] = entry.T.astype(BF)

    loads[6].wait()
    loads[7].wait()
    own_part(feat)
    back_through(2, cot)
    spread(False)

    arrived(0)
    unpack(0)
    forward(0, h1)
    gather(h1, 3)
    exchange(3)
    own_part(h1)

    arrived(1)
    unpack(1)
    forward(1, h2)
    gather(h2, 4)
    exchange(4, 1, HELD)

    weight_grad(1, grad)
    back_through(1, grad)
    spread(True)
    x_stage(1)
    weight_grad(0, grad)
    own_part(h2)
    x_stage(0)

    arrived(2)
    unpack(2)
    forward(2, emb)
    weight_grad(2, cot)
    y_stage(1)
    x_stage(2)
    y_stage(0)
    z_prepare(1)
    y_stage(2)
    z_prepare(0)
    z_prepare(2)
    for s in range(1, N_Z):
        z_copy(s).start()
    exchange(4, HELD, N_DOM)
    for s in range(1, N_Z):
        z_copy(s).wait_recv()
    total = z_out[z].astype(F32)
    for s in range(1, N_Z):
        total = total + z_in[s - 1].astype(F32)
    quarters[g] = total * (1.0 / math.sqrt(N_GRP * N_DOM * ROWS))
    for s in range(1, N_GRP):
        q_copy(s).start()

    for s in range(1, N_GRP):
        q_copy(s).wait_recv()
    for q in range(N_GRP):
        wg_o[:, :, q * 128:(q + 1) * 128] = quarters[q]

    arrived(3)
    arrived(4)
    for turn in range(5):
        block = send.at[turn, pl.ds(0, N_DOM - 1)]
        pltpu.make_async_copy(block, block, send_sem.at[turn]).wait()
    for layer in range(3):
        core_copy(layer).wait_send()
        for s in range(1, N_GRP):
            x_copy(layer, s).wait_send()
        for s in range(1, N_Y):
            y_copy(layer, s).wait_send()
    for s in range(1, N_Z):
        z_copy(s).wait_send()
    for s in range(1, N_GRP):
        q_copy(s).wait_send()


def out_kernel(emb, fresh, grads, emb_o, fresh_o, grads_o, sem):
    copies = [
        pltpu.make_async_copy(a, b, sem.at[i])
        for i, (a, b) in enumerate([(emb, emb_o), (fresh, fresh_o), (grads, grads_o)])
    ]
    for copy in copies:
        copy.start()
    for copy in copies:
        copy.wait()


def body(features, history, adj_tiles, blocks, send_list, counts, weights, cotangent):
    vmem = pltpu.VMEM
    dma = pltpu.SemaphoreType.DMA
    whole = pl.BlockSpec(memory_space=vmem)
    anywhere = pl.BlockSpec(memory_space=pl.ANY)
    shapes = (((ROWS, D), BF), ((2, N_DOM, CAP, D), BF), ((3, 8, D), F32))
    made = pl.pallas_call(
        step_kernel,
        out_shape=tuple(vmem(*shape) for shape in shapes),
        in_specs=[pl.BlockSpec(memory_space=pltpu.SMEM)] + [anywhere] * 7,
        out_specs=(whole,) * 3,
        scratch_shapes=[
            vmem((CAP, N_DOM), jnp.int32),
            vmem((1, N_DOM), jnp.int32),
            vmem((ROWS, D), BF),
            vmem((2, ROWS, D), BF),
            vmem((8, 4, 128, 128), BF),
            vmem((3, D, D), BF),
            vmem((ROWS, D), BF),
            vmem((HALO, ROWS), BF),
            vmem((ROWS, ROWS + HALO), BF),
            vmem((ROWS, ROWS), BF),
            vmem((HALO, D), BF),
            vmem((ROWS, D), BF),
            vmem((ROWS, D), BF),
            vmem((3, ROWS, D), BF),
            vmem((ROWS, D), F32),
            vmem((ROWS, D), F32),
            vmem((ROWS, D), F32),
            vmem((ROWS, D), BF),
            vmem((ROWS, D), BF),
            vmem((5, N_DOM, CAP, D), BF),
            vmem((3, N_DOM, CAP, D), BF),
            vmem((3, 32, 2, 8, D), BF),
            vmem((3, 32, 8, D), BF),
            vmem((N_GRP, 3, 32, 8, 128), BF),
            vmem((N_GRP - 1, 3, 32, 8, 128), BF),
            vmem((N_Y, 3, N_Z, 8, 128), BF),
            vmem((N_Y - 1, 3, N_Z, 8, 128), BF),
            vmem((N_Z, 3, 8, 128), BF),
            vmem((N_Z - 1, 3, 8, 128), BF),
            vmem((N_GRP, 3, 8, 128), F32),
            dma((8,)),
            dma((5,)),
            dma((5,)),
            dma((2, 3)),
            dma((2, 3, N_GRP - 1)),
            dma((2, 3, N_Y - 1)),
            dma((2, N_Z - 1)),
            dma((2, N_GRP - 1)),
        ],
        compiler_params=pltpu.CompilerParams(
            collective_id=0, has_side_effects=True, vmem_limit_bytes=56 << 20
        ),
        name="graph_step",
    )(
        blocks[0].T, send_list[0, 0].T, counts[0], features[0], history[:, 0], adj_tiles[0], weights, cotangent[0]
    )
    made = [pltpu.with_memory_space_constraint(piece, pltpu.VMEM) for piece in made]
    embedding, fresh, grads = pl.pallas_call(
        out_kernel,
        out_shape=tuple(jax.ShapeDtypeStruct(*shape) for shape in shapes),
        in_specs=[whole] * 3,
        out_specs=(anywhere,) * 3,
        scratch_shapes=[dma((3,))],
        name="outputs",
    )(*made)
    return (embedding[None], fresh.reshape(2, 1, HALO, D), grads)


def solution(mesh):
    placed = (
        P("grp", "dom", None),
        P(None, "grp", "dom", None),
        P("grp", "dom", None, None, None),
        P("grp", "dom", None),
        P("grp", "dom", None, None),
        P("grp", "dom", None),
        P(),
        P("grp", "dom", None),
    )
    return jax.shard_map(
        body,
        mesh=mesh,
        in_specs=placed,
        out_specs=(P("grp", "dom", None), P(None, "grp", "dom", None), P(None, "dom", None)),
        check_vma=False,
    )
```
